512 devices in a mesh: prow: 32 (over y, x, core), pcol: 16 (over z).
Axes of the slice: x: 4, y: 4, z: 16, core: 2. Of those that a mesh axis runs over, the one named last changes fastest.
Arguments:
- inverse_blocks: bfloat16 [128, 128, 128, 128], P('pcol', 'prow'), may hold values from -6 to 6
- lower_blocks: bfloat16 [128, 4, 128, 128], P('prow', None, 'pcol'), may hold values from -0.625 to 0.625
- pattern: int32 [4, 64], replicated, may hold values from 0 to 127, as said below
- diag_inverse: float32 [4, 16384], P(None, ('prow', 'pcol')), may hold values from -6 to 6
Outputs:
- inverse_column: float32 [128, 4, 128, 128], P('pcol', None, 'prow')
- inverse_diag: float32 [4, 16384], P(None, ('prow', 'pcol'))
The draws below stay inside these ranges and needn't reach their ends.
Inputs may be any that keep to these rules, and one draw needn't show every extreme that they name: `pattern`: each row names 64 different ancestor blocks.
All inputs are finite; a program needn't handle non-finite values.
Results may differ from the reference program's by a relative error of at most 0.0003.
Values may be sent and summed in bfloat16 or wider, within the bound.
A program may use at most 64 MiB of HBM per device.

```python
import jax
import jax.numpy as jnp
from jax import lax

B = 128
NK = 4
G = 128
P_SIZE = 64


def draw_pattern(key, part):
    node_keys = jax.random.split(key, NK)
    picked = jax.vmap(lambda single: jax.random.permutation(single, G)[:P_SIZE])(node_keys)
    return picked.astype(jnp.int32)


def strengthened(result, rng, source, target, blocks, factor):
    def block_of(axis_at):
        return (jnp.arange(result.shape[axis_at]) // (result.shape[axis_at] // blocks)).reshape((-1,) + (1,) * (result.ndim - 1 - axis_at))

    one_side = jax.random.permutation(rng, blocks)[block_of(target)]
    other_side = (block_of(target) + blocks // 2) % blocks
    return jnp.where((block_of(source) == one_side) | (block_of(source) == other_side), factor * result, result)


def levels(own_key, extent, pieces, low, largest):
    level = 1.0
    for position, shards_of in pieces:
        steps = jax.random.uniform(jax.random.fold_in(jax.random.fold_in(own_key, 6), position), (shards_of,), jnp.float32, low / len(pieces), largest / len(pieces))
        level = level * jnp.repeat(jnp.exp(steps), extent[position] // shards_of).reshape((-1,) + (1,) * (len(extent) - 1 - position))
    return level


def bell_draw(own_key, extent, width, reach, pieces=(), kind=jnp.bfloat16):
    drawn = jax.random.normal(own_key, extent, jnp.float32) * width
    if len(pieces) > 0:
        drawn = levels(own_key, extent, pieces, -0.22, 0.18) * drawn
    return jnp.clip(drawn, min=-reach, max=reach).astype(kind)


def bell_draw_with(own_key, shape, width, most, cuts, heavy, held_as=jnp.bfloat16):
    entries = width * jax.random.normal(own_key, shape, jnp.float32)
    if cuts:
        entries = entries * levels(own_key, shape, cuts, -0.22, 0.18)
    return jnp.clip(strengthened(entries, jax.random.fold_in(own_key, 3), *heavy), -most, most).astype(held_as)


def setup_inputs(seed: int = 0) -> dict:
    keys = jax.random.split(jax.random.key(seed), 5)
    return {
        "inverse_blocks": bell_draw_with(keys[0], (G, G, B, B), ((P_SIZE * B) ** -0.15), 6.0, ((0, 16), (1, 32)), (1, 2, 32, 2.75)),
        "lower_blocks": bell_draw(keys[1], (G, NK, B, B), ((P_SIZE * B) ** -0.35), 0.625, ((0, 32), (2, 16))),
        "pattern": draw_pattern(jax.random.fold_in(keys[4], 71), 0),
        "diag_inverse": bell_draw(keys[3], (NK, B * B), 1.0, 6.0, ((1, 512),), jnp.float32),
    }


def reference(inverse_blocks, lower_blocks, pattern, diag_inverse):
    block_count = inverse_blocks.shape[0]
    node_count = lower_blocks.shape[1]
    block_width = lower_blocks.shape[3]
    matches = pattern[None, :, :] == jnp.arange(block_count, dtype=jnp.int32)[:, None, None]
    present = jnp.sum(matches.astype(jnp.float32), axis=2)
    masked = lower_blocks * present.astype(jnp.bfloat16)[:, :, None, None]
    masked_wide = masked.astype(jnp.float32)

    def one_block(packed):
        row_blocks, keep_col, own_lower = packed
        products = jnp.einsum("jrb,jkbe->kre", row_blocks.astype(jnp.float32), masked_wide, precision=lax.Precision.HIGHEST)
        column = -keep_col[:, None, None] * products
        partial_value = jnp.einsum("kra,krb->kab", own_lower, column, precision=lax.Precision.HIGHEST)
        return column, partial_value

    columns, partials = lax.map(one_block, (inverse_blocks, present, masked_wide))
    update = jnp.sum(partials, axis=0).reshape(node_count, block_width * block_width)
    return columns, diag_inverse - update
```

```python
import jax
import jax.numpy as jnp
from jax import lax
from jax.sharding import PartitionSpec as P


def per_device(inverse_blocks, lower_blocks, pattern, diag_inverse):
    blocks_i = inverse_blocks.shape[0]
    blocks_j = inverse_blocks.shape[1]
    block_width = inverse_blocks.shape[3]
    node_count = lower_blocks.shape[1]
    row_groups = lax.axis_size("prow")
    col_groups = lax.axis_size("pcol")
    block_count = blocks_j * row_groups
    ratio = row_groups // col_groups
    row_share = block_width // row_groups
    p = lax.axis_index("prow")
    c = lax.axis_index("pcol")
    matches = pattern[None, :, :] == jnp.arange(block_count, dtype=jnp.int32)[:, None, None]
    present = jnp.sum(matches.astype(jnp.float32), axis=2)
    keep_j = lax.dynamic_slice_in_dim(present, p * blocks_j, blocks_j, 0)
    keep_i = lax.dynamic_slice_in_dim(present, c * blocks_i, blocks_i, 0)
    shard = lower_blocks * keep_j.astype(jnp.bfloat16)[:, :, None, None]
    pieces = []
    for flip in range(ratio):
        moves = [
            ((ratio * q + k) * col_groups + z, (ratio * z + (k ^ flip)) * col_groups + q)
            for q in range(col_groups)
            for k in range(ratio)
            for z in range(col_groups)
        ]
        start = ((p % ratio) ^ flip) * row_share
        piece = lax.dynamic_slice_in_dim(shard, start, row_share, 2)
        pieces.append(lax.ppermute(piece, ("prow", "pcol"), moves))
    whole = lax.all_gather(lower_blocks, "pcol", axis=2, tiled=True)
    masked = whole * keep_j.astype(jnp.bfloat16)[:, :, None, None]
    summed = lax.psum_scatter(
        jnp.einsum("ijrb,jkbe->rike", inverse_blocks, masked, preferred_element_type=jnp.float32),
        "prow",
        scatter_dimension=0,
        tiled=True,
    )
    column = summed * (-keep_i)[None, :, :, None]
    first = (p % ratio) == 0
    own_lower = jnp.concatenate(
        [jnp.where(first, pieces[0], pieces[1]), jnp.where(first, pieces[1], pieces[0])], axis=0
    )
    partial_value = jnp.einsum(
        "ikra,rikb->kab", own_lower.astype(jnp.float32), column, precision=lax.Precision.HIGHEST
    )
    partial_value = partial_value.reshape(node_count, block_width * block_width)
    diag_piece = lax.psum_scatter(partial_value, ("prow", "pcol"), scatter_dimension=1, tiled=True)
    return (jnp.transpose(column, (1, 2, 0, 3)), diag_inverse - diag_piece)


def solution(mesh):
    placed = (
        P("pcol", "prow", None, None),
        P("prow", None, "pcol", None),
        P(),
        P(None, ("prow", "pcol")),
    )
    return jax.shard_map(
        per_device,
        mesh=mesh,
        in_specs=placed,
        out_specs=(P("pcol", None, "prow", None), P(None, ("prow", "pcol"))),
        check_vma=False,
    )
```

```python
import functools

import jax
import jax.numpy as jnp
from jax import lax
from jax.experimental import pallas as pl
from jax.experimental.pallas import tpu as pltpu
from jax.sharding import PartitionSpec as P

MESH = pl.DeviceIdType.MESH
F32 = jnp.float32
BF16 = jnp.bfloat16
STRIDE = 2


def kernel(
    inv, low, pat, col_out, upd_out,
    invs, lg, lown, rhs, pbuf, t1, d1, s1, c1, q1, t2, d2, s2, c2, cs, ubuf, urecv, wbuf, wrecv,
    inv_send, inv_recv, own_sem, ag_send, ag_recv, pt_send, pt_recv, low_send, low_recv,
    p1_send, p1_recv, p2_send, p2_recv, col_send, col_recv, col_local, u_send, u_recv, w_send, w_recv,
    row_sem, col_sem,
):
    p = lax.axis_index("prow")
    z = lax.axis_index("pcol")
    k = lax.rem(p, 2)
    q = lax.div(p, 2)
    x = lax.rem(q, 4)
    y = lax.div(q, 4)
    other = 1 - k

    def dev(yy, xx, kk, zz):
        return (lax.rem(yy + 8, 4) * 8 + lax.rem(xx + 8, 4) * 2 + kk, lax.rem(zz + 32, 16))

    def chip(qq, kk, zz):
        return (qq * 2 + kk, zz)

    partner = dev(y, x, other, z)

    def remote(src, dst, send, recv, to):
        return pltpu.make_async_remote_copy(
            src_ref=src, dst_ref=dst, send_sem=send, recv_sem=recv, device_id=to, device_id_type=MESH
        )

    def signal(sem, to):
        pl.semaphore_signal(sem, inc=1, device_id=to, device_id_type=MESH)

    barrier = pltpu.get_barrier_semaphore()
    near = [partner, dev(y, x + 1, k, z), dev(y, x - 1, k, z), dev(y + 1, x, k, z), dev(y - 1, x, k, z)]
    for hop in range(1, STRIDE + 1):
        near += [dev(y, x, k, z + hop), dev(y, x, k, z - hop)]
    for to in near:
        signal(barrier, to)
    pl.semaphore_wait(barrier, len(near))

    def rows(zz, first=0, count=4):
        return (pl.ds(4 * k + first, count), slice(None), pl.ds(pl.multiple_of(8 * zz, 8), 8), slice(None))

    sends = []

    def spread(src, piece, d, way, s):
        for hop in range(STRIDE, 0, -1):
            t = d + hop
            if t > 8:
                continue
            if STRIDE == 2 and d % 2 == 1:
                continue
            if t == 8:
                src_at, dst_at = src(2 * way, 2), piece(2 * way, 2)
            else:
                src_at, dst_at = src(0, 4), piece(0, 4)
            c = remote(src_at, dst_at, ag_send.at[way, t], ag_recv.at[way, t], dev(y, x, k, z + s * hop))
            c.start()
            sends.append(c)

    ways = ((0, 1), (1, -1))
    for way, s in ways:
        spread(lambda f, n: low.at[pl.ds(f, n)], lambda f, n: lg.at[rows(z, f, n)], 0, way, s)
    inv_out = remote(
        inv.at[pl.ds(4 * other, 4)], invs.at[:, pl.ds(4 * k, 4)], inv_send, inv_recv, partner
    )
    own_out = remote(low, lg.at[rows(z)], pt_send.at[0, 0], pt_recv.at[0, 0], partner)
    own_out.start()
    inv_out.start()
    own_in = pltpu.make_async_copy(low, lg.at[rows(z)], own_sem.at[0])
    own_in.start()
    inv_in = pltpu.make_async_copy(inv.at[pl.ds(4 * k, 4)], invs.at[:, pl.ds(4 * k, 4)], own_sem.at[1])
    inv_in.start()
    root = q == z

    @pl.when(root)
    def _():
        pltpu.make_async_copy(low, lown, low_recv).start()

    signal(row_sem, dev(y, x + 1, k, z))
    signal(row_sem, dev(y, x - 1, k, z))
    pl.semaphore_wait(row_sem, 2)
    for lap in range(2):
        signal(col_sem.at[lap], dev(y + 1, x, k, z))
        signal(col_sem.at[lap], dev(y - 1, x, k, z))
        pl.semaphore_wait(col_sem.at[lap], 2)

    forwards = [own_out]
    scatters = []

    def arrive(d):
        for way, s in ways:
            from_z = lax.rem(z - s * d + 32, 16)
            if d == 8:
                got = lg.at[rows(from_z, 2 * way, 2)]
            else:
                got = lg.at[rows(from_z)]
            remote(got, got, ag_send.at[way, d], ag_recv.at[way, d], partner).wait_recv()
            here = lambda f, n, fz=from_z: lg.at[rows(fz, f, n)]
            spread(here, here, d, way, s)
            c = remote(got, got, pt_send.at[way, d], pt_recv.at[way, d], partner)
            c.start()
            forwards.append(c)
            if d < 8 or way == 1:
                c = remote(
                    lg.at[rows(from_z)], lown, low_send.at[way, d], low_recv, chip(from_z, k, z)
                )
                scatters.append(c)
                pl.when(root)(c.start)

    order = (2, 1, 4, 3, 6, 5, 8, 7) if STRIDE == 2 else tuple(range(1, 9))
    for d in order:
        arrive(d)

    def rows_of(kk, zz, first, count):
        return (pl.ds(4 * kk + first, count), slice(None), pl.ds(pl.multiple_of(8 * zz, 8), 8), slice(None))

    got = lg.at[rows_of(other, z, 0, 4)]
    remote(got, got, pt_send.at[0, 0], pt_recv.at[0, 0], partner).wait_recv()
    for d in order:
        for way, s in ways:
            from_z = lax.rem(z - s * d + 32, 16)
            got = lg.at[rows_of(other, from_z, 2 * way, 2)] if d == 8 else lg.at[rows_of(other, from_z, 0, 4)]
            remote(got, got, pt_send.at[way, d], pt_recv.at[way, d], partner).wait_recv()
    own_in.wait()
    inv_in.wait()
    inv_out.wait_recv()

    def present(g):
        return jnp.sum((pat[...] == g).astype(F32), axis=1, keepdims=True)

    for j in range(8):
        keep = present(8 * q + j)
        for n in range(4):
            keep_n = jnp.broadcast_to(keep[n : n + 1, :], (128, 128)).astype(BF16)
            rhs[128 * j : 128 * (j + 1), 128 * n : 128 * (n + 1)] = lg[j, n] * keep_n

    def part(h, i, m):
        return pbuf.at[i, :, m] if h == 0 else pbuf.at[i, m]

    def mod4(v):
        return lax.rem(v + 8, 4)

    def ring(h, step):
        return (x if (h == 0) == (step == 1) else y)

    def ring_dev(h, step, by):
        return dev(y, x + by, k, z) if (h == 0) == (step == 1) else dev(y + by, x, k, z)

    reduces = []

    def begin(h, way, s, step, chunk, t, d, send, recv):
        n = ring(h, step)
        for what, src, dst, by in (
            (0, chunk(mod4(n + 2 * s)), t, s),
            (1, chunk(mod4(n - s)), d, -s),
        ):
            c = remote(src, dst.at[h, way], send.at[h, way, what], recv.at[h, way, what], ring_dev(h, step, by))
            c.start()
            reduces.append(c)

    def combine(h, way, s, step, chunk, t, sbuf, cbuf, send, recv):
        n = ring(h, step)
        ref = t.at[h, way]
        remote(ref, ref, send.at[h, way, 0], recv.at[h, way, 0], partner).wait_recv()
        sbuf[h, way] = t[h, way] + chunk(mod4(n + s))[...]
        c = remote(sbuf.at[h, way], cbuf.at[h, way], send.at[h, way, 2], recv.at[h, way, 2], ring_dev(h, step, s))
        c.start()
        reduces.append(c)

    def finish(h, way, step, chunk, d, cbuf, send, recv):
        n = ring(h, step)
        ref = d.at[h, way]
        remote(ref, ref, send.at[h, way, 1], recv.at[h, way, 1], partner).wait_recv()
        ref = cbuf.at[h, way]
        remote(ref, ref, send.at[h, way, 2], recv.at[h, way, 2], partner).wait_recv()
        return chunk(n)[...] + d[h, way] + cbuf[h, way]

    pairs = [(h, way, s) for way, s in ways for h in range(2)]
    for h, way, s in pairs:
        i = 2 * h + way
        lhs = jnp.concatenate([invs[i, j] for j in range(8)], axis=1)
        prod = jnp.dot(lhs, rhs[...], preferred_element_type=F32)
        pbuf[i] = prod.reshape(4, 4, 8, 512)
        begin(h, way, s, 1, functools.partial(part, h, i), t1, d1, p1_send, p1_recv)
    for h, way, s in pairs:
        combine(h, way, s, 1, functools.partial(part, h, 2 * h + way), t1, s1, c1, p1_send, p1_recv)
    for h, way, s in pairs:
        q1[h, way] = finish(h, way, 1, functools.partial(part, h, 2 * h + way), d1, c1, p1_send, p1_recv)
        begin(h, way, s, 2, lambda m, h=h, way=way: q1.at[h, way, m], t2, d2, p2_send, p2_recv)
    for h, way, s in pairs:
        combine(h, way, s, 2, lambda m, h=h, way=way: q1.at[h, way, m], t2, s2, c2, p2_send, p2_recv)
    columns = [None] * 4
    for h, way, s in pairs:
        i = 2 * h + way
        total = finish(h, way, 2, lambda m, h=h, way=way: q1.at[h, way, m], d2, c2, p2_send, p2_recv)
        keep = present(8 * z + 4 * k + i)
        keep_row = jnp.concatenate([jnp.broadcast_to(keep[n : n + 1, :], (8, 128)) for n in range(4)], axis=1)
        columns[i] = -keep_row * total

    remote(lown, lown, low_send.at[0, 0], low_recv, partner).wait_recv()
    for n in range(4):
        left = lown[:, n].astype(F32).reshape(32, 128)
        right = jnp.concatenate([columns[i][:, 128 * n : 128 * (n + 1)] for i in range(4)], axis=0)
        prod = lax.dot_general(
            left, right, (((0,), (0,)), ((), ())), precision=lax.Precision.HIGHEST, preferred_element_type=F32
        )
        ubuf[n] = prod.reshape(16, 8, 128)

    def u_copy(step):
        to = lax.rem(q + step, 16)
        return remote(ubuf.at[:, to], urecv.at[step], u_send.at[step], u_recv.at[step], chip(to, k, z))

    @pl.loop(1, 16)
    def _(step):
        u_copy(step).start()

    for half in range(2):
        for i in range(4):
            for n in range(4):
                cs[half, i, n] = columns[i][4 * half : 4 * half + 4, 128 * n : 128 * (n + 1)]
    col_move = pltpu.make_async_copy(cs.at[k], col_out.at[pl.ds(4 * k, 4)], col_local)
    col_move.start()
    col_pass = remote(cs.at[other], col_out.at[pl.ds(4 * k, 4)], col_send, col_recv, partner)
    col_pass.start()

    value = ubuf[:, q]
    for step in range(1, 16):
        u_copy(step).wait_recv()
        value = value + urecv[step]

    group = lax.broadcasted_iota(jnp.int32, (8, 128), 1) // 32
    for m in range(4):
        packed = jnp.zeros((8, 128), F32)
        for n in range(4):
            turned = value[n] if n == m else pltpu.roll(value[n], (32 * (n - m)) % 128, 1)
            packed = jnp.where(group == n, turned, packed)
        for r in range(8):
            wbuf[r // 4, 4 * (r % 4) + m] = packed[r : r + 1, :]

    def w_copy(flip, step):
        kk = k if flip == 0 else other
        zz = lax.rem(z + step, 16)
        return remote(
            wbuf.at[kk, zz], wrecv.at[flip, step], w_send.at[flip, step], w_recv.at[flip, step], chip(q, kk, zz)
        )

    w_copy(1, 0).start()

    @pl.loop(1, 16)
    def _(step):
        w_copy(0, step).start()
        w_copy(1, step).start()

    inv_out.wait_send()
    for c in sends + forwards + reduces:
        c.wait_send()
    for c in scatters:
        pl.when(root)(c.wait_send)

    @pl.loop(1, 16)
    def _(step):
        u_copy(step).wait_send()

    col_move.wait()
    col_pass.wait()

    total = wbuf[k, z]
    w_copy(1, 0).wait_recv()
    total = total + wrecv[1, 0]
    for step in range(1, 16):
        for flip in range(2):
            w_copy(flip, step).wait_recv()
            total = total + wrecv[flip, step]
    upd_out[...] = total
    w_copy(1, 0).wait_send()

    @pl.loop(1, 16)
    def _(step):
        w_copy(0, step).wait_send()
        w_copy(1, step).wait_send()


def per_device(inverse_blocks, lower_blocks, pattern, diag_inverse):
    any_spec = pl.BlockSpec(memory_space=pl.ANY)
    vmem_spec = pl.BlockSpec(memory_space=pltpu.VMEM)
    dma = pltpu.SemaphoreType.DMA
    column, update = pl.pallas_call(
        kernel,
        out_shape=(
            jax.ShapeDtypeStruct((8, 4, 4, 128), F32),
            jax.ShapeDtypeStruct((1, 128), F32),
        ),
        in_specs=[any_spec, any_spec, vmem_spec],
        out_specs=(any_spec, vmem_spec),
        scratch_shapes=[
            pltpu.VMEM((4, 8, 128, 128), BF16),
            pltpu.VMEM((8, 4, 128, 128), BF16),
            pltpu.VMEM((4, 4, 8, 128), BF16),
            pltpu.VMEM((1024, 512), BF16),
            pltpu.VMEM((4, 4, 4, 8, 512), F32),
            pltpu.VMEM((2, 2, 4, 8, 512), F32),
            pltpu.VMEM((2, 2, 4, 8, 512), F32),
            pltpu.VMEM((2, 2, 4, 8, 512), F32),
            pltpu.VMEM((2, 2, 4, 8, 512), F32),
            pltpu.VMEM((2, 2, 4, 8, 512), F32),
            pltpu.VMEM((2, 2, 8, 512), F32),
            pltpu.VMEM((2, 2, 8, 512), F32),
            pltpu.VMEM((2, 2, 8, 512), F32),
            pltpu.VMEM((2, 2, 8, 512), F32),
            pltpu.VMEM((2, 4, 4, 4, 128), F32),
            pltpu.VMEM((4, 16, 8, 128), F32),
            pltpu.VMEM((16, 4, 8, 128), F32),
            pltpu.VMEM((2, 16, 1, 128), F32),
            pltpu.VMEM((2, 16, 1, 128), F32),
            dma, dma, dma((2,)),
            dma((2, 9)), dma((2, 9)),
            dma((2, 9)), dma((2, 9)),
            dma((2, 9)), dma,
            dma((2, 2, 3)), dma((2, 2, 3)),
            dma((2, 2, 3)), dma((2, 2, 3)),
            dma, dma, dma,
            dma((16,)), dma((16,)),
            dma((2, 16)), dma((2, 16)),
            pltpu.SemaphoreType.REGULAR, pltpu.SemaphoreType.REGULAR((2,)),
        ],
        compiler_params=pltpu.CompilerParams(
            collective_id=0, has_side_effects=True, vmem_limit_bytes=32 * 1024 * 1024
        ),
    )(inverse_blocks, lower_blocks, pattern)
    return column, diag_inverse - update.reshape(4, 32)


def solution(mesh):
    placed = (
        P("pcol", "prow", None, None),
        P("prow", None, "pcol", None),
        P(),
        P(None, ("prow", "pcol")),
    )
    return jax.shard_map(
        per_device,
        mesh=mesh,
        in_specs=placed,
        out_specs=(P("pcol", None, "prow", None), P(None, ("prow", "pcol"))),
        check_vma=False,
    )
```

```python
import functools

import jax
import jax.numpy as jnp
from jax import lax
from jax.experimental import pallas as pl
from jax.experimental.pallas import tpu as pltpu
from jax.sharding import PartitionSpec as P

MESH = pl.DeviceIdType.MESH
F32 = jnp.float32
BF16 = jnp.bfloat16
TREE = {0: ((3, 3), (1, 1)), 3: ((6, 3), (4, 1), (2, -1)), 6: ((8, 2), (7, 1), (5, -1))}


def kernel(
    inv, low, pat_in, diag_in, col_out, upd_out,
    pat, diag,
    invs, lg, lown, rhs, pbuf, t1, d1, s1, c1, q1, t2, d2, s2, c2, cs, ubuf, urecv, wbuf, wrecv,
    inv_send, inv_recv, own_sem, ag_send, ag_recv, pt_send, pt_recv, low_send, low_recv,
    p1_send, p1_recv, p2_send, p2_recv, col_send, col_recv, col_local, u_send, u_recv, w_send, w_recv,
    row_sem, col_sem,
):
    p = lax.axis_index("prow")
    z = lax.axis_index("pcol")
    k = lax.rem(p, 2)
    q = lax.div(p, 2)
    x = lax.rem(q, 4)
    y = lax.div(q, 4)
    other = 1 - k

    def dev(yy, xx, kk, zz):
        return (lax.rem(yy + 8, 4) * 8 + lax.rem(xx + 8, 4) * 2 + kk, lax.rem(zz + 32, 16))

    def chip(qq, kk, zz):
        return (qq * 2 + kk, zz)

    partner = dev(y, x, other, z)

    def remote(src, dst, send, recv, to):
        return pltpu.make_async_remote_copy(
            src_ref=src, dst_ref=dst, send_sem=send, recv_sem=recv, device_id=to, device_id_type=MESH
        )

    def signal(sem, to):
        pl.semaphore_signal(sem, inc=1, device_id=to, device_id_type=MESH)

    barrier = pltpu.get_barrier_semaphore()
    near = [partner, dev(y, x + 1, k, z), dev(y, x - 1, k, z), dev(y + 1, x, k, z), dev(y - 1, x, k, z)]
    for hop in range(1, 4):
        near += [dev(y, x, k, z + hop), dev(y, x, k, z - hop)]
    for to in near:
        signal(barrier, to)
    pl.semaphore_wait(barrier, len(near))

    def rows(zz, first=0, count=4):
        return (k, zz, pl.ds(first, count))

    sends = []

    def spread(src, piece, d, way, s):
        for t, hop in TREE.get(d, ()):
            if t == 8:
                src_at, dst_at = src(2 * way, 2), piece(2 * way, 2)
            else:
                src_at, dst_at = src(0, 4), piece(0, 4)
            c = remote(src_at, dst_at, ag_send.at[way, t], ag_recv.at[way, t], dev(y, x, k, z + s * hop))
            c.start()
            sends.append(c)

    ways = ((0, 1), (1, -1))
    for way, s in ways:
        spread(lambda f, n: low.at[pl.ds(f, n)], lambda f, n: lg.at[rows(z, f, n)], 0, way, s)
    inv_out = remote(
        inv.at[pl.ds(4 * other, 4)], invs.at[:, pl.ds(4 * k, 4)], inv_send, inv_recv, partner
    )
    own_out = remote(low, lg.at[rows(z)], pt_send.at[0, 0], pt_recv.at[0, 0], partner)
    own_out.start()
    inv_out.start()
    own_in = pltpu.make_async_copy(low, lg.at[rows(z)], own_sem.at[0])
    own_in.start()
    inv_in = pltpu.make_async_copy(inv.at[pl.ds(4 * k, 4)], invs.at[:, pl.ds(4 * k, 4)], own_sem.at[1])
    inv_in.start()
    pat_move = pltpu.make_async_copy(pat_in, pat, own_sem.at[2])
    pat_move.start()
    diag_move = pltpu.make_async_copy(diag_in, diag, own_sem.at[3])
    diag_move.start()
    root = q == z

    @pl.when(root)
    def _():
        pltpu.make_async_copy(low, lown, low_recv).start()

    signal(row_sem, dev(y, x + 1, k, z))
    signal(row_sem, dev(y, x - 1, k, z))
    pl.semaphore_wait(row_sem, 2)
    for lap in range(2):
        signal(col_sem.at[lap], dev(y + 1, x, k, z))
        signal(col_sem.at[lap], dev(y - 1, x, k, z))
        pl.semaphore_wait(col_sem.at[lap], 2)

    forwards = [own_out]
    scatters = []

    def arrive(d):
        for way, s in ways:
            from_z = lax.rem(z - s * d + 32, 16)
            if d == 8:
                got = lg.at[rows(from_z, 2 * way, 2)]
            else:
                got = lg.at[rows(from_z)]
            remote(got, got, ag_send.at[way, d], ag_recv.at[way, d], partner).wait_recv()
            here = lambda f, n, fz=from_z: lg.at[rows(fz, f, n)]
            spread(here, here, d, way, s)
            c = remote(got, got, pt_send.at[way, d], pt_recv.at[way, d], partner)
            c.start()
            forwards.append(c)
            if d < 8 or way == 1:
                c = remote(
                    lg.at[rows(from_z)], lown, low_send.at[way, d], low_recv, chip(from_z, k, z)
                )
                scatters.append(c)
                pl.when(root)(c.start)

    order = (3, 1, 6, 4, 2, 7, 5, 8)
    for d in order:
        arrive(d)


    def drain_ag():
        inv_out.wait_send()
        for c in sends + forwards:
            c.wait_send()
        for c in scatters:
            pl.when(root)(c.wait_send)

    def rows_of(kk, zz, first, count):
        return (kk, zz, pl.ds(first, count))

    got = lg.at[rows_of(other, z, 0, 4)]
    remote(got, got, pt_send.at[0, 0], pt_recv.at[0, 0], partner).wait_recv()
    for d in order:
        for way, s in ways:
            from_z = lax.rem(z - s * d + 32, 16)
            got = lg.at[rows_of(other, from_z, 2 * way, 2)] if d == 8 else lg.at[rows_of(other, from_z, 0, 4)]
            remote(got, got, pt_send.at[way, d], pt_recv.at[way, d], partner).wait_recv()
    own_in.wait()
    inv_in.wait()
    pat_move.wait()
    diag_move.wait()
    inv_out.wait_recv()

    def present(g):
        return jnp.sum((pat[...] == g).astype(F32), axis=1, keepdims=True)

    for j in range(8):
        keep = present(8 * q + j)
        for n in range(4):
            keep_n = jnp.broadcast_to(keep[n : n + 1, :], (128, 128))
            block = lg[j // 4, :, j % 4, n].astype(F32).reshape(128, 128)
            rhs[128 * j : 128 * (j + 1), 128 * n : 128 * (n + 1)] = (block * keep_n).astype(BF16)

    def part(h, i, m):
        return pbuf.at[i, :, m] if h == 0 else pbuf.at[i, m]

    def mod4(v):
        return lax.rem(v + 8, 4)

    def ring(h, step):
        return (x if (h == 0) == (step == 1) else y)

    def ring_dev(h, step, by):
        return dev(y, x + by, k, z) if (h == 0) == (step == 1) else dev(y + by, x, k, z)

    reduces = []

    def begin(h, way, s, step, chunk, t, d, send, recv):
        n = ring(h, step)
        for what, src, dst, by in (
            (0, chunk(mod4(n + 2 * s)), t, s),
            (1, chunk(mod4(n - s)), d, -s),
        ):
            c = remote(src, dst.at[h, way], send.at[h, way, what], recv.at[h, way, what], ring_dev(h, step, by))
            c.start()
            reduces.append(c)

    def combine(h, way, s, step, chunk, t, sbuf, cbuf, send, recv):
        n = ring(h, step)
        ref = t.at[h, way]
        remote(ref, ref, send.at[h, way, 0], recv.at[h, way, 0], partner).wait_recv()
        sbuf[h, way] = t[h, way] + chunk(mod4(n + s))[...]
        c = remote(sbuf.at[h, way], cbuf.at[h, way], send.at[h, way, 2], recv.at[h, way, 2], ring_dev(h, step, s))
        c.start()
        reduces.append(c)

    def finish(h, way, step, chunk, d, cbuf, send, recv):
        n = ring(h, step)
        ref = d.at[h, way]
        remote(ref, ref, send.at[h, way, 1], recv.at[h, way, 1], partner).wait_recv()
        ref = cbuf.at[h, way]
        remote(ref, ref, send.at[h, way, 2], recv.at[h, way, 2], partner).wait_recv()
        return chunk(n)[...] + d[h, way] + cbuf[h, way]

    pairs = [(h, way, s) for way, s in ways for h in range(2)]
    for h, way, s in pairs:
        i = 2 * h + way
        lhs = jnp.concatenate([invs[i, j] for j in range(8)], axis=1)
        prod = jnp.dot(lhs, rhs[...], preferred_element_type=F32)
        pbuf[i] = prod.reshape(4, 4, 8, 512)
        begin(h, way, s, 1, functools.partial(part, h, i), t1, d1, p1_send, p1_recv)
    for h, way, s in pairs:
        combine(h, way, s, 1, functools.partial(part, h, 2 * h + way), t1, s1, c1, p1_send, p1_recv)
    for h, way, s in pairs:
        q1[h, way] = finish(h, way, 1, functools.partial(part, h, 2 * h + way), d1, c1, p1_send, p1_recv)
        begin(h, way, s, 2, lambda m, h=h, way=way: q1.at[h, way, m], t2, d2, p2_send, p2_recv)
    for h, way, s in pairs:
        combine(h, way, s, 2, lambda m, h=h, way=way: q1.at[h, way, m], t2, s2, c2, p2_send, p2_recv)
    columns = [None] * 4
    for h, way, s in pairs:
        i = 2 * h + way
        total = finish(h, way, 2, lambda m, h=h, way=way: q1.at[h, way, m], d2, c2, p2_send, p2_recv)
        keep = present(8 * z + 4 * k + i)
        keep_row = jnp.concatenate([jnp.broadcast_to(keep[n : n + 1, :], (8, 128)) for n in range(4)], axis=1)
        columns[i] = -keep_row * total

    remote(lown, lown, low_send.at[0, 0], low_recv, partner).wait_recv()
    for n in range(4):
        left = lown[:, n].astype(F32).reshape(32, 128)
        right = jnp.concatenate([columns[i][:, 128 * n : 128 * (n + 1)] for i in range(4)], axis=0)
        prod = lax.dot_general(
            left, right, (((0,), (0,)), ((), ())), precision=lax.Precision.HIGHEST, preferred_element_type=F32
        )
        ubuf[n] = prod.reshape(16, 8, 128)

    def u_copy(step):
        to = lax.rem(q + step, 16)
        return remote(ubuf.at[:, to], urecv.at[step], u_send.at[step], u_recv.at[step], chip(to, k, z))

    @pl.loop(1, 16)
    def _(step):
        u_copy(step).start()

    for half in range(2):
        for i in range(4):
            for n in range(4):
                cs[half, i, n] = columns[i][4 * half : 4 * half + 4, 128 * n : 128 * (n + 1)]
    col_move = pltpu.make_async_copy(cs.at[k], col_out.at[pl.ds(4 * k, 4)], col_local)
    col_move.start()
    col_pass = remote(cs.at[other], col_out.at[pl.ds(4 * k, 4)], col_send, col_recv, partner)
    col_pass.start()

    value = ubuf[:, q]
    for step in range(1, 16):
        u_copy(step).wait_recv()
        value = value + urecv[step]

    group = lax.broadcasted_iota(jnp.int32, (8, 128), 1) // 32
    for m in range(4):
        packed = jnp.zeros((8, 128), F32)
        for n in range(4):
            turned = value[n] if n == m else pltpu.roll(value[n], (32 * (n - m)) % 128, 1)
            packed = jnp.where(group == n, turned, packed)
        for r in range(8):
            wbuf[r // 4, 4 * (r % 4) + m] = packed[r : r + 1, :]

    def w_copy(flip, step):
        kk = k if flip == 0 else other
        zz = lax.rem(z + step, 16)
        return remote(
            wbuf.at[kk, zz], wrecv.at[flip, step], w_send.at[flip, step], w_recv.at[flip, step], chip(q, kk, zz)
        )

    w_copy(1, 0).start()

    @pl.loop(1, 16)
    def _(step):
        w_copy(0, step).start()
        w_copy(1, step).start()

    inv_out.wait_send()
    for c in sends + forwards + reduces:
        c.wait_send()
    for c in scatters:
        pl.when(root)(c.wait_send)

    @pl.loop(1, 16)
    def _(step):
        u_copy(step).wait_send()

    col_move.wait()
    col_pass.wait()

    total = wbuf[k, z]
    w_copy(1, 0).wait_recv()
    total = total + wrecv[1, 0]
    for step in range(1, 16):
        for flip in range(2):
            w_copy(flip, step).wait_recv()
            total = total + wrecv[flip, step]
    for n in range(4):
        upd_out[n : n + 1, :] = diag[n : n + 1, :] - total[:, 32 * n : 32 * (n + 1)]
    w_copy(1, 0).wait_send()

    @pl.loop(1, 16)
    def _(step):
        w_copy(0, step).wait_send()
        w_copy(1, step).wait_send()


def per_device(inverse_blocks, lower_blocks, pattern, diag_inverse):
    any_spec = pl.BlockSpec(memory_space=pltpu.HBM)
    vmem_spec = pl.BlockSpec(memory_space=pltpu.VMEM)
    dma = pltpu.SemaphoreType.DMA
    column, update = pl.pallas_call(
        kernel,
        out_shape=(
            pltpu.VMEM((8, 4, 4, 128), F32),
            pltpu.VMEM((4, 32), F32),
        ),
        in_specs=[any_spec] * 4,
        out_specs=(vmem_spec, vmem_spec),
        scratch_shapes=[
            pltpu.VMEM((4, 64), jnp.int32), pltpu.VMEM((4, 32), F32),
            pltpu.VMEM((4, 8, 128, 128), BF16),
            pltpu.VMEM((2, 16, 4, 4, 8, 128), BF16),
            pltpu.VMEM((4, 4, 8, 128), BF16),
            pltpu.VMEM((1024, 512), BF16),
            pltpu.VMEM((4, 4, 4, 8, 512), F32),
            pltpu.VMEM((2, 2, 4, 8, 512), F32),
            pltpu.VMEM((2, 2, 4, 8, 512), F32),
            pltpu.VMEM((2, 2, 4, 8, 512), F32),
            pltpu.VMEM((2, 2, 4, 8, 512), F32),
            pltpu.VMEM((2, 2, 4, 8, 512), F32),
            pltpu.VMEM((2, 2, 8, 512), F32),
            pltpu.VMEM((2, 2, 8, 512), F32),
            pltpu.VMEM((2, 2, 8, 512), F32),
            pltpu.VMEM((2, 2, 8, 512), F32),
            pltpu.VMEM((2, 4, 4, 4, 128), F32),
            pltpu.VMEM((4, 16, 8, 128), F32),
            pltpu.VMEM((16, 4, 8, 128), F32),
            pltpu.VMEM((2, 16, 1, 128), F32),
            pltpu.VMEM((2, 16, 1, 128), F32),
            dma, dma, dma((4,)),
            dma((2, 9)), dma((2, 9)),
            dma((2, 9)), dma((2, 9)),
            dma((2, 9)), dma,
            dma((2, 2, 3)), dma((2, 2, 3)),
            dma((2, 2, 3)), dma((2, 2, 3)),
            dma, dma, dma,
            dma((16,)), dma((16,)),
            dma((2, 16)), dma((2, 16)),
            pltpu.SemaphoreType.REGULAR, pltpu.SemaphoreType.REGULAR((2,)),
        ],
        compiler_params=pltpu.CompilerParams(
            collective_id=0, has_side_effects=True
        ),
    )(inverse_blocks, lower_blocks, pattern, diag_inverse)
    return column, update


def solution(mesh):
    placed = (
        P("pcol", "prow", None, None),
        P("prow", None, "pcol", None),
        P(),
        P(None, ("prow", "pcol")),
    )
    return jax.shard_map(
        per_device,
        mesh=mesh,
        in_specs=placed,
        out_specs=(P("pcol", None, "prow", None), P(None, ("prow", "pcol"))),
        check_vma=False,
    )
```

```python
import functools

import jax
import jax.numpy as jnp
from jax import lax
from jax.experimental import pallas as pl
from jax.experimental.pallas import tpu as pltpu
from jax.sharding import PartitionSpec as P

MESH = pl.DeviceIdType.MESH
F32 = jnp.float32
BF16 = jnp.bfloat16
TREE = {0: ((3, 3), (1, 1)), 3: ((6, 3), (4, 1), (2, -1)), 6: ((8, 2), (7, 1), (5, -1))}


def kernel(
    inv, low, pat_in, diag_in, col_out, upd_out,
    pat, diag,
    invs, lg, lown, rhs, pbuf, t1, d1, s1, c1, q1, t2, d2, s2, c2, cs, lring, ubuf, urecv, wbuf, wrecv,
    inv_send, inv_recv, own_sem, ag_send, ag_recv, pt_send, pt_recv, low_send, low_recv,
    p1_send, p1_recv, p2_send, p2_recv, col_send, col_recv, col_local, lr_send, lr_recv, u_send, u_recv, w_send, w_recv,
    row_sem, col_sem,
):
    p = lax.axis_index("prow")
    z = lax.axis_index("pcol")
    k = lax.rem(p, 2)
    q = lax.div(p, 2)
    x = lax.rem(q, 4)
    y = lax.div(q, 4)
    other = 1 - k

    def dev(yy, xx, kk, zz):
        return (lax.rem(yy + 8, 4) * 8 + lax.rem(xx + 8, 4) * 2 + kk, lax.rem(zz + 32, 16))

    def chip(qq, kk, zz):
        return (qq * 2 + kk, zz)

    partner = dev(y, x, other, z)

    def remote(src, dst, send, recv, to):
        return pltpu.make_async_remote_copy(
            src_ref=src, dst_ref=dst, send_sem=send, recv_sem=recv, device_id=to, device_id_type=MESH
        )

    def signal(sem, to):
        pl.semaphore_signal(sem, inc=1, device_id=to, device_id_type=MESH)

    barrier = pltpu.get_barrier_semaphore()
    near = [partner, dev(y, x + 1, k, z), dev(y, x - 1, k, z), dev(y + 1, x, k, z), dev(y - 1, x, k, z)]
    for hop in range(1, 4):
        near += [dev(y, x, k, z + hop), dev(y, x, k, z - hop)]
    for to in near:
        signal(barrier, to)
    pl.semaphore_wait(barrier, len(near))

    def rows(zz, first=0, count=4):
        return (k, zz, pl.ds(first, count))

    sends = []

    def spread(src, piece, d, way, s):
        for t, hop in TREE.get(d, ()):
            if t == 8:
                src_at, dst_at = src(2 * way, 2), piece(2 * way, 2)
            else:
                src_at, dst_at = src(0, 4), piece(0, 4)
            c = remote(src_at, dst_at, ag_send.at[way, t], ag_recv.at[way, t], dev(y, x, k, z + s * hop))
            c.start()
            sends.append(c)

    ways = ((0, 1), (1, -1))
    for way, s in ways:
        spread(lambda f, n: low.at[pl.ds(f, n)], lambda f, n: lg.at[rows(z, f, n)], 0, way, s)
    inv_out = remote(
        inv.at[pl.ds(4 * other, 4)], invs.at[:, pl.ds(4 * k, 4)], inv_send, inv_recv, partner
    )
    own_out = remote(low, lg.at[rows(z)], pt_send.at[0, 0], pt_recv.at[0, 0], partner)
    own_out.start()
    inv_out.start()
    own_in = pltpu.make_async_copy(low, lg.at[rows(z)], own_sem.at[0])
    own_in.start()
    inv_in = pltpu.make_async_copy(inv.at[pl.ds(4 * k, 4)], invs.at[:, pl.ds(4 * k, 4)], own_sem.at[1])
    inv_in.start()
    pat_move = pltpu.make_async_copy(pat_in, pat, own_sem.at[2])
    pat_move.start()
    diag_move = pltpu.make_async_copy(diag_in, diag, own_sem.at[3])
    diag_move.start()
    root = q == z

    @pl.when(root)
    def _():
        pltpu.make_async_copy(low, lown, low_recv).start()

    signal(row_sem, dev(y, x + 1, k, z))
    signal(row_sem, dev(y, x - 1, k, z))
    pl.semaphore_wait(row_sem, 2)
    for lap in range(2):
        signal(col_sem.at[lap], dev(y + 1, x, k, z))
        signal(col_sem.at[lap], dev(y - 1, x, k, z))
        pl.semaphore_wait(col_sem.at[lap], 2)

    forwards = [own_out]
    scatters = []

    def arrive(d):
        for way, s in ways:
            from_z = lax.rem(z - s * d + 32, 16)
            if d == 8:
                got = lg.at[rows(from_z, 2 * way, 2)]
            else:
                got = lg.at[rows(from_z)]
            remote(got, got, ag_send.at[way, d], ag_recv.at[way, d], partner).wait_recv()
            here = lambda f, n, fz=from_z: lg.at[rows(fz, f, n)]
            spread(here, here, d, way, s)
            c = remote(got, got, pt_send.at[way, d], pt_recv.at[way, d], partner)
            c.start()
            forwards.append(c)
            if d < 8 or way == 1:
                c = remote(
                    lg.at[rows(from_z)], lown, low_send.at[way, d], low_recv, chip(from_z, k, z)
                )
                scatters.append(c)
                pl.when(root)(c.start)

    order = (3, 1, 6, 4, 2, 7, 5, 8)
    for d in order:
        arrive(d)


    def drain_ag():
        inv_out.wait_send()
        for c in sends + forwards:
            c.wait_send()
        for c in scatters:
            pl.when(root)(c.wait_send)

    def rows_of(kk, zz, first, count):
        return (kk, zz, pl.ds(first, count))

    got = lg.at[rows_of(other, z, 0, 4)]
    remote(got, got, pt_send.at[0, 0], pt_recv.at[0, 0], partner).wait_recv()
    for d in order:
        for way, s in ways:
            from_z = lax.rem(z - s * d + 32, 16)
            got = lg.at[rows_of(other, from_z, 2 * way, 2)] if d == 8 else lg.at[rows_of(other, from_z, 0, 4)]
            remote(got, got, pt_send.at[way, d], pt_recv.at[way, d], partner).wait_recv()
    own_in.wait()
    inv_in.wait()
    pat_move.wait()
    diag_move.wait()
    inv_out.wait_recv()

    def present(g):
        return jnp.sum((pat[...] == g).astype(F32), axis=1, keepdims=True)

    for j in range(8):
        keep = present(8 * q + j)
        for n in range(4):
            keep_n = jnp.broadcast_to(keep[n : n + 1, :], (128, 128))
            block = lg[j // 4, :, j % 4, n].astype(F32).reshape(128, 128)
            rhs[128 * j : 128 * (j + 1), 128 * n : 128 * (n + 1)] = (block * keep_n).astype(BF16)

    def part(h, i, m):
        return pbuf.at[i, :, m] if h == 0 else pbuf.at[i, m]

    def mod4(v):
        return lax.rem(v + 8, 4)

    def ring(h, step):
        return (x if (h == 0) == (step == 1) else y)

    def ring_dev(h, step, by):
        return dev(y, x + by, k, z) if (h == 0) == (step == 1) else dev(y + by, x, k, z)

    reduces = []

    def begin(h, way, s, step, chunk, t, d, send, recv):
        n = ring(h, step)
        for what, src, dst, by in (
            (0, chunk(mod4(n + 2 * s)), t, s),
            (1, chunk(mod4(n - s)), d, -s),
        ):
            c = remote(src, dst.at[h, way], send.at[h, way, what], recv.at[h, way, what], ring_dev(h, step, by))
            c.start()
            reduces.append(c)

    def combine(h, way, s, step, chunk, t, sbuf, cbuf, send, recv):
        n = ring(h, step)
        ref = t.at[h, way]
        remote(ref, ref, send.at[h, way, 0], recv.at[h, way, 0], partner).wait_recv()
        sbuf[h, way] = t[h, way] + chunk(mod4(n + s))[...]
        c = remote(sbuf.at[h, way], cbuf.at[h, way], send.at[h, way, 2], recv.at[h, way, 2], ring_dev(h, step, s))
        c.start()
        reduces.append(c)

    def finish(h, way, step, chunk, d, cbuf, send, recv):
        n = ring(h, step)
        ref = d.at[h, way]
        remote(ref, ref, send.at[h, way, 1], recv.at[h, way, 1], partner).wait_recv()
        ref = cbuf.at[h, way]
        remote(ref, ref, send.at[h, way, 2], recv.at[h, way, 2], partner).wait_recv()
        return chunk(n)[...] + d[h, way] + cbuf[h, way]

    pairs = [(h, way, s) for way, s in ways for h in range(2)]
    for h, way, s in pairs:
        i = 2 * h + way
        lhs = jnp.concatenate([invs[i, j] for j in range(8)], axis=1)
        prod = jnp.dot(lhs, rhs[...], preferred_element_type=F32)
        pbuf[i] = prod.reshape(4, 4, 8, 512)
        begin(h, way, s, 1, functools.partial(part, h, i), t1, d1, p1_send, p1_recv)
    for h, way, s in pairs:
        combine(h, way, s, 1, functools.partial(part, h, 2 * h + way), t1, s1, c1, p1_send, p1_recv)

    remote(lown, lown, low_send.at[0, 0], low_recv, partner).wait_recv()
    mine = (y, x)
    shares = []
    for h in range(2):
        c = pltpu.make_async_copy(lown.at[pl.ds(2 * h, 2)], lring.at[h, :, mine[h]], lr_recv.at[h, 0])
        c.start()
        for by in (2, 1, 3):
            to = dev(y + by, x, k, z) if h == 0 else dev(y, x + by, k, z)
            c = remote(lown.at[pl.ds(2 * h, 2)], lring.at[h, :, mine[h]], lr_send.at[h, by], lr_recv.at[h, by], to)
            c.start()
            shares.append(c)
    for h, way, s in pairs:
        q1[h, way] = finish(h, way, 1, functools.partial(part, h, 2 * h + way), d1, c1, p1_send, p1_recv)
        begin(h, way, s, 2, lambda m, h=h, way=way: q1.at[h, way, m], t2, d2, p2_send, p2_recv)
    for h in range(2):
        for by in range(4):
            ref = lring.at[h, :, mod4(mine[h] - by)]
            if by == 0:
                pltpu.make_async_copy(lown.at[pl.ds(2 * h, 2)], ref, lr_recv.at[h, 0]).wait()
            else:
                remote(ref, ref, lr_send.at[h, by], lr_recv.at[h, by], partner).wait_recv()
    keeps = [present(8 * z + 4 * k + i) for i in range(4)]
    for n in range(4):
        left = lring[:, :, :, n].astype(F32).reshape(128, 128)
        right = jnp.concatenate(
            [
                -jnp.broadcast_to(keeps[2 * h + way][n : n + 1, :], (32, 128))
                * q1[h, way, :, :, 128 * n : 128 * (n + 1)].reshape(32, 128)
                for h in range(2)
                for way in range(2)
            ],
            axis=0,
        )
        prod = lax.dot_general(
            left, right, (((0,), (0,)), ((), ())), precision=lax.Precision.HIGHEST, preferred_element_type=F32
        )
        ubuf[n] = prod.reshape(16, 8, 128)

    def u_copy(dy, dx):
        to_y, to_x = mod4(y + dy), mod4(x + dx)
        slot = 4 * dy + dx
        return remote(
            ubuf.at[:, 4 * to_y + to_x], urecv.at[slot], u_send.at[slot], u_recv.at[slot], dev(to_y, to_x, k, z)
        )

    far = (0, 1, 2, 1)
    u_order = sorted(((dy, dx) for dy in range(4) for dx in range(4) if dy + dx), key=lambda v: -far[v[0]] - far[v[1]])
    u_sends = [u_copy(dy, dx) for dy, dx in u_order]
    for c in u_sends:
        c.start()

    for h, way, s in pairs:
        combine(h, way, s, 2, lambda m, h=h, way=way: q1.at[h, way, m], t2, s2, c2, p2_send, p2_recv)
    columns = [None] * 4
    for h, way, s in pairs:
        i = 2 * h + way
        total = finish(h, way, 2, lambda m, h=h, way=way: q1.at[h, way, m], d2, c2, p2_send, p2_recv)
        keep = keeps[i]
        keep_row = jnp.concatenate([jnp.broadcast_to(keep[n : n + 1, :], (8, 128)) for n in range(4)], axis=1)
        columns[i] = -keep_row * total

    for half in range(2):
        for i in range(4):
            for n in range(4):
                cs[half, i, n] = columns[i][4 * half : 4 * half + 4, 128 * n : 128 * (n + 1)]
    col_move = pltpu.make_async_copy(cs.at[k], col_out.at[pl.ds(4 * k, 4)], col_local)
    col_move.start()
    col_pass = remote(cs.at[other], col_out.at[pl.ds(4 * k, 4)], col_send, col_recv, partner)
    col_pass.start()

    value = ubuf[:, q]
    for (dy, dx), c in zip(reversed(u_order), reversed(u_sends), strict=True):
        c.wait_recv()
        value = value + urecv[4 * dy + dx]

    group = lax.broadcasted_iota(jnp.int32, (8, 128), 1) // 32
    for m in range(4):
        packed = jnp.zeros((8, 128), F32)
        for n in range(4):
            turned = value[n] if n == m else pltpu.roll(value[n], (32 * (n - m)) % 128, 1)
            packed = jnp.where(group == n, turned, packed)
        for r in range(8):
            wbuf[r // 4, 4 * (r % 4) + m] = packed[r : r + 1, :]

    def w_copy(flip, step):
        kk = k if flip == 0 else other
        zz = lax.rem(z + step, 16)
        return remote(
            wbuf.at[kk, zz], wrecv.at[flip, step], w_send.at[flip, step], w_recv.at[flip, step], chip(q, kk, zz)
        )

    w_order = [(flip, step) for step in sorted(range(1, 16), key=lambda v: -min(v, 16 - v)) for flip in range(2)] + [(1, 0)]
    w_sends = [w_copy(flip, step) for flip, step in w_order]
    for c in w_sends:
        c.start()

    inv_out.wait_send()
    for c in sends + forwards + reduces + shares + u_sends:
        c.wait_send()
    for c in scatters:
        pl.when(root)(c.wait_send)

    col_move.wait()
    col_pass.wait()

    total = wbuf[k, z]
    for (flip, step), c in zip(reversed(w_order), reversed(w_sends), strict=True):
        c.wait_recv()
        total = total + wrecv[flip, step]
    for n in range(4):
        upd_out[n : n + 1, :] = diag[n : n + 1, :] - total[:, 32 * n : 32 * (n + 1)]
    for c in w_sends:
        c.wait_send()


def per_device(inverse_blocks, lower_blocks, pattern, diag_inverse):
    any_spec = pl.BlockSpec(memory_space=pltpu.HBM)
    vmem_spec = pl.BlockSpec(memory_space=pltpu.VMEM)
    dma = pltpu.SemaphoreType.DMA
    column, update = pl.pallas_call(
        kernel,
        out_shape=(
            pltpu.VMEM((8, 4, 4, 128), F32),
            pltpu.VMEM((4, 32), F32),
        ),
        in_specs=[any_spec] * 4,
        out_specs=(vmem_spec, vmem_spec),
        scratch_shapes=[
            pltpu.VMEM((4, 64), jnp.int32), pltpu.VMEM((4, 32), F32),
            pltpu.VMEM((4, 8, 128, 128), BF16),
            pltpu.VMEM((2, 16, 4, 4, 8, 128), BF16),
            pltpu.VMEM((4, 4, 8, 128), BF16),
            pltpu.VMEM((1024, 512), BF16),
            pltpu.VMEM((4, 4, 4, 8, 512), F32),
            pltpu.VMEM((2, 2, 4, 8, 512), F32),
            pltpu.VMEM((2, 2, 4, 8, 512), F32),
            pltpu.VMEM((2, 2, 4, 8, 512), F32),
            pltpu.VMEM((2, 2, 4, 8, 512), F32),
            pltpu.VMEM((2, 2, 4, 8, 512), F32),
            pltpu.VMEM((2, 2, 8, 512), F32),
            pltpu.VMEM((2, 2, 8, 512), F32),
            pltpu.VMEM((2, 2, 8, 512), F32),
            pltpu.VMEM((2, 2, 8, 512), F32),
            pltpu.VMEM((2, 4, 4, 4, 128), F32),
            pltpu.VMEM((2, 2, 4, 4, 8, 128), BF16),
            pltpu.VMEM((4, 16, 8, 128), F32),
            pltpu.VMEM((16, 4, 8, 128), F32),
            pltpu.VMEM((2, 16, 1, 128), F32),
            pltpu.VMEM((2, 16, 1, 128), F32),
            dma, dma, dma((4,)),
            dma((2, 9)), dma((2, 9)),
            dma((2, 9)), dma((2, 9)),
            dma((2, 9)), dma,
            dma((2, 2, 3)), dma((2, 2, 3)),
            dma((2, 2, 3)), dma((2, 2, 3)),
            dma, dma, dma,
            dma((2, 4)), dma((2, 4)),
            dma((16,)), dma((16,)),
            dma((2, 16)), dma((2, 16)),
            pltpu.SemaphoreType.REGULAR, pltpu.SemaphoreType.REGULAR((2,)),
        ],
        compiler_params=pltpu.CompilerParams(
            collective_id=0, has_side_effects=True
        ),
    )(inverse_blocks, lower_blocks, pattern, diag_inverse)
    return column, update


def solution(mesh):
    placed = (
        P("pcol", "prow", None, None),
        P("prow", None, "pcol", None),
        P(),
        P(None, ("prow", "pcol")),
    )
    return jax.shard_map(
        per_device,
        mesh=mesh,
        in_specs=placed,
        out_specs=(P("pcol", None, "prow", None), P(None, ("prow", "pcol"))),
        check_vma=False,
    )
```

```python
import functools

import jax
import jax.numpy as jnp
from jax import lax
from jax.experimental import pallas as pl
from jax.experimental.pallas import tpu as pltpu
from jax.sharding import PartitionSpec as P

MESH = pl.DeviceIdType.MESH
F32 = jnp.float32
BF16 = jnp.bfloat16
TREE = {0: ((3, 3), (1, 1)), 3: ((6, 3), (4, 1), (2, -1)), 6: ((8, 2), (7, 1), (5, -1))}

NW = 2
NN = 4 // NW
LANES = 512 // NW


def kernel(
    inv, low, pat_in, diag_in, col_out, upd_out,
    pat, diag,
    invs, lg, lown, rhs, masks, pbuf, t1, d1, s1, c1, q1, t2, d2, s2, c2, cs, lring, ubuf, urecv, wbuf, wrecv,
    sized, near_send, pass_send, sum_send, low_send, w_send,
    own_sem, pat_sem, ag_recv, pt_recv, low_recv, t1_recv, p1_recv, t2_recv, p2_recv, lr_recv, col_recv, u_recv, w_recv,
    row_sem, col_sem,
):
    p = lax.axis_index("prow")
    z = lax.axis_index("pcol")
    k = lax.rem(p, 2)
    q = lax.div(p, 2)
    x = lax.rem(q, 4)
    y = lax.div(q, 4)
    other = 1 - k

    def dev(yy, xx, kk, zz):
        return (lax.rem(yy + 8, 4) * 8 + lax.rem(xx + 8, 4) * 2 + kk, lax.rem(zz + 32, 16))

    def chip(qq, kk, zz):
        return (qq * 2 + kk, zz)

    partner = dev(y, x, other, z)

    def remote(src, dst, send, recv, to):
        return pltpu.make_async_remote_copy(
            src_ref=src, dst_ref=dst, send_sem=send, recv_sem=recv, device_id=to, device_id_type=MESH
        )

    def await_kib(sem, count):
        ref = sized.at[pl.ds(0, count)]
        pltpu.make_async_copy(ref, ref, sem).wait()

    def signal(sem, to):
        pl.semaphore_signal(sem, inc=1, device_id=to, device_id_type=MESH)

    barrier = pltpu.get_barrier_semaphore()
    near = [partner, dev(y, x + 1, k, z), dev(y, x - 1, k, z), dev(y + 1, x, k, z), dev(y - 1, x, k, z)]
    for hop in range(1, 4):
        near += [dev(y, x, k, z + hop), dev(y, x, k, z - hop)]
    for to in near:
        signal(barrier, to)
    pl.semaphore_wait(barrier, len(near))

    def rows(kk, zz, wave, first=0, count=4):
        return (
            pl.ds(4 * kk + first, count), pl.ds(NN * wave, NN), pl.ds(pl.multiple_of(8 * zz, 8), 8), slice(None)
        )

    def spread(zz, d, way, s, wave, held):
        for t, hop in TREE.get(d, ()):
            first, count = (2 * way, 2) if t == 8 else (0, 4)
            src = lg.at[rows(k, zz, wave, first, count)] if held else low.at[:, pl.ds(NN * wave, NN)]
            c = remote(
                src, lg.at[rows(k, zz, wave, first, count)],
                near_send, ag_recv.at[way, t - 1, wave], dev(y, x, k, z + s * hop),
            )
            yield c

    ways = ((0, 1), (1, -1))
    starts = [[list(spread(z, 0, way, s, wave, False)) for way, s in ways] for wave in range(NW)]
    for hop in range(2):
        for wave in range(NW):
            for way, _ in ways:
                starts[wave][way][hop].start()
    inv_out = remote(
        inv.at[pl.ds(4 * other, 4)], invs.at[:, pl.ds(4 * k, 4)], pass_send, pt_recv.at[0], partner
    )
    whole = (pl.ds(4 * k, 4), slice(None), pl.ds(pl.multiple_of(8 * z, 8), 8), slice(None))
    own_out = remote(low, lg.at[whole], pass_send, pt_recv.at[0], partner)
    own_out.start()
    inv_out.start()
    own_in = pltpu.make_async_copy(low, lg.at[whole], own_sem)
    own_in.start()
    inv_in = pltpu.make_async_copy(inv.at[pl.ds(4 * k, 4)], invs.at[:, pl.ds(4 * k, 4)], own_sem)
    inv_in.start()
    pat_move = pltpu.make_async_copy(pat_in, pat, pat_sem.at[0])
    pat_move.start()
    diag_move = pltpu.make_async_copy(diag_in, diag, pat_sem.at[1])
    diag_move.start()
    root = q == z

    @pl.when(root)
    def _():
        pltpu.make_async_copy(low, lown, low_recv).start()

    signal(row_sem, dev(y, x + 1, k, z))
    signal(row_sem, dev(y, x - 1, k, z))
    pl.semaphore_wait(row_sem, 2)
    for lap in range(2):
        signal(col_sem.at[lap], dev(y + 1, x, k, z))
        signal(col_sem.at[lap], dev(y - 1, x, k, z))
        pl.semaphore_wait(col_sem.at[lap], 2)

    def present(g):
        return jnp.broadcast_to(jnp.sum((pat[...] == g).astype(F32), axis=1, keepdims=True), (4, 128))

    pat_move.wait()
    for j in range(8):
        masks[j] = present(8 * q + j)
    for i in range(4):
        masks[8 + i] = present(8 * z + 4 * k + i)


    def arrive(d, wave):
        for way, s in ways:
            from_z = lax.rem(z - s * d + 32, 16)
            got = lg.at[rows(k, from_z, wave, 2 * way, 2)] if d == 8 else lg.at[rows(k, from_z, wave)]
            pltpu.make_async_copy(got, got, ag_recv.at[way, d - 1, wave]).wait()
            for c in spread(from_z, d, way, s, wave, True):
                c.start()
            c = remote(got, got, pass_send, pt_recv.at[wave], partner)
            c.start()
            if wave == NW - 1 and (d < 8 or way == 1):
                piece = (pl.ds(4 * k, 4), slice(None), pl.ds(pl.multiple_of(8 * from_z, 8), 8), slice(None))
                c = remote(lg.at[piece], lown, low_send, low_recv, chip(from_z, k, z))
                pl.when(root)(c.start)

    order = (3, 1, 6, 4, 2, 7, 5, 8)

    def part(h, i, wave, m):
        lanes = pl.ds(LANES * wave, LANES)
        return pbuf.at[i, :, m, :, lanes] if h == 0 else pbuf.at[i, m, :, :, lanes]

    def mod4(v):
        return lax.rem(v + 8, 4)

    def ring(h, step):
        return (x if (h == 0) == (step == 1) else y)

    def ring_dev(h, step, by):
        return dev(y, x + by, k, z) if (h == 0) == (step == 1) else dev(y + by, x, k, z)

    def begin(h, way, s, step, chunk, t, d, t_sem, sem):
        n = ring(h, step)
        remote(chunk(mod4(n + 2 * s)), t, sum_send, t_sem, ring_dev(h, step, s)).start()
        remote(chunk(mod4(n - s)), d, sum_send, sem, ring_dev(h, step, -s)).start()

    def combine(h, way, s, step, chunk, t, sbuf, cbuf, sem):
        n = ring(h, step)
        sbuf[...] = t[...] + chunk(mod4(n + s))[...]
        remote(sbuf, cbuf, sum_send, sem, ring_dev(h, step, s)).start()

    def finish(h, step, chunk, d, cbuf):
        return chunk(ring(h, step))[...] + d[...] + cbuf[...]

    pairs = [(h, way, s) for way, s in ways for h in range(2)]

    def product(wave):
        for j in range(8):
            for n in range(NN * wave, NN * wave + NN):
                keep = jnp.broadcast_to(masks[j, n : n + 1, :], (128, 128)).astype(BF16)
                rhs[wave, 128 * j : 128 * (j + 1), 128 * (n % NN) : 128 * (n % NN + 1)] = lg[j, n] * keep
        for way, s in ways:
            lhs = jnp.concatenate(
                [jnp.concatenate([invs[2 * h + way, j] for j in range(8)], axis=1) for h in range(2)], axis=0
            )
            prod = jnp.dot(lhs, rhs[wave], preferred_element_type=F32)
            for h in range(2):
                i = 2 * h + way
                pbuf[i, :, :, :, LANES * wave : LANES * (wave + 1)] = prod[128 * h : 128 * (h + 1)].reshape(4, 4, 8, LANES)
                begin(
                    h, way, s, 1, functools.partial(part, h, i, wave),
                    t1.at[wave, h, way], d1.at[wave, h, way], t1_recv.at[wave, h, way], p1_recv.at[wave],
                )

    for d in order[:5]:
        for wave in range(NW):
            arrive(d, wave)
    diag_move.wait()
    for wave in range(NW):
        for d in order[5:]:
            arrive(d, wave)
        if wave == 0:
            await_kib(own_sem, 32 + 512)
        await_kib(pt_recv.at[wave], 30 * 16 // NW + (32 + 512 if wave == 0 else 0))
        product(wave)
    for wave in range(NW):
        for h, way, s in pairs:
            await_kib(t1_recv.at[wave, h, way], 64 // NW)
            combine(
                h, way, s, 1, functools.partial(part, h, 2 * h + way, wave),
                t1.at[wave, h, way], s1.at[wave, h, way], c1.at[wave, h, way], p1_recv.at[wave],
            )

    pltpu.make_async_copy(lown, lown, low_recv).wait()
    mine = (y, x)
    for h in range(2):
        c = pltpu.make_async_copy(lown.at[pl.ds(2 * h, 2)], lring.at[h, :, mine[h]], lr_recv)
        c.start()
        for by in (2, 1, 3):
            to = dev(y + by, x, k, z) if h == 0 else dev(y, x + by, k, z)
            c = remote(lown.at[pl.ds(2 * h, 2)], lring.at[h, :, mine[h]], near_send, lr_recv, to)
            c.start()
    for wave in range(NW):
        await_kib(p1_recv.at[wave], 512 // NW)
    for h, way, s in pairs:
        for wave in range(NW):
            q1[h, way, :, :, LANES * wave : LANES * (wave + 1)] = finish(
                h, 1, functools.partial(part, h, 2 * h + way, wave), d1.at[wave, h, way], c1.at[wave, h, way]
            )
        begin(
            h, way, s, 2, lambda m, h=h, way=way: q1.at[h, way, m], t2.at[h, way], d2.at[h, way], t2_recv, p2_recv
        )
    await_kib(lr_recv, 128)
    for n in range(4):
        left = lring[:, :, :, n].astype(F32).reshape(128, 128)
        right = jnp.concatenate(
            [
                -jnp.broadcast_to(masks[8 + 2 * h + way, n : n + 1, :], (32, 128))
                * q1[h, way, :, :, 128 * n : 128 * (n + 1)].reshape(32, 128)
                for h in range(2)
                for way in range(2)
            ],
            axis=0,
        )
        prod = lax.dot_general(
            left, right, (((0,), (0,)), ((), ())), precision=lax.Precision.HIGHEST, preferred_element_type=F32
        )
        ubuf[n] = prod.reshape(16, 8, 128)

    def u_copy(dy, dx):
        to_y, to_x = mod4(y + dy), mod4(x + dx)
        slot = 4 * dy + dx - 1
        return remote(
            ubuf.at[:, 4 * to_y + to_x], urecv.at[slot], near_send, u_recv, dev(to_y, to_x, k, z)
        )

    far = (0, 1, 2, 1)
    u_order = sorted(((dy, dx) for dy in range(4) for dx in range(4) if dy + dx), key=lambda v: -far[v[0]] - far[v[1]])
    u_sends = [u_copy(dy, dx) for dy, dx in u_order]
    for c in u_sends:
        c.start()

    await_kib(t2_recv, 64)
    for h, way, s in pairs:
        combine(h, way, s, 2, lambda m, h=h, way=way: q1.at[h, way, m],
            t2.at[h, way], s2.at[h, way], c2.at[h, way], p2_recv)
    await_kib(p2_recv, 128)
    columns = [None] * 4
    for h, way, s in pairs:
        i = 2 * h + way
        total = finish(h, 2, lambda m, h=h, way=way: q1.at[h, way, m],
            d2.at[h, way], c2.at[h, way])
        keep_row = jnp.concatenate(
            [jnp.broadcast_to(masks[8 + i, n : n + 1, :], (8, 128)) for n in range(4)], axis=1
        )
        columns[i] = -keep_row * total

    for half in range(2):
        for i in range(4):
            for n in range(4):
                cs[half, i, n] = columns[i][4 * half : 4 * half + 4, 128 * n : 128 * (n + 1)]
    col_move = pltpu.make_async_copy(cs.at[k], col_out.at[pl.ds(4 * k, 4)], col_recv.at[0])
    col_move.start()
    col_pass = remote(cs.at[other], col_out.at[pl.ds(4 * k, 4)], near_send, col_recv.at[1], partner)
    col_pass.start()

    value = ubuf[:, q]
    await_kib(u_recv, 240)
    for slot in range(15):
        value = value + urecv[slot]

    group = lax.broadcasted_iota(jnp.int32, (8, 128), 1) // 32
    for m in range(4):
        packed = jnp.zeros((8, 128), F32)
        for n in range(4):
            turned = value[n] if n == m else pltpu.roll(value[n], (32 * (n - m)) % 128, 1)
            packed = jnp.where(group == n, turned, packed)
        for r in range(8):
            wbuf[r // 4, 4 * (r % 4) + m] = packed[r : r + 1, :]

    def w_copy(flip, step):
        kk = k if flip == 0 else other
        zz = lax.rem(z + step, 16)
        return remote(
            wbuf.at[kk, zz], wrecv.at[16 * flip + step - 1], w_send, w_recv, chip(q, kk, zz)
        )

    w_order = [(flip, step) for step in sorted(range(1, 16), key=lambda v: -min(v, 16 - v)) for flip in range(2)] + [(1, 0)]
    w_sends = [w_copy(flip, step) for flip, step in w_order]
    for c in w_sends:
        c.start()

    await_kib(near_send, 480 + 96 + 240 + 32)
    await_kib(pass_send, 512 + 512)
    await_kib(sum_send, 768 + 192)

    @pl.when(root)
    def _():
        await_kib(low_send, 480)

    col_move.wait()
    col_pass.wait_recv()

    pltpu.make_async_copy(wrecv, wrecv, w_recv).wait()
    total = wbuf[k, z]
    for slot in range(31):
        total = total + wrecv[slot]
    for n in range(4):
        upd_out[n : n + 1, :] = diag[n : n + 1, :] - total[:, 32 * n : 32 * (n + 1)]
    pltpu.make_async_copy(wrecv, wrecv, w_send).wait()


def per_device(inverse_blocks, lower_blocks, pattern, diag_inverse):
    any_spec = pl.BlockSpec(memory_space=pltpu.HBM)
    vmem_spec = pl.BlockSpec(memory_space=pltpu.VMEM)
    dma = pltpu.SemaphoreType.DMA
    column, update = pl.pallas_call(
        kernel,
        out_shape=(
            pltpu.VMEM((8, 4, 4, 128), F32),
            pltpu.VMEM((4, 32), F32),
        ),
        in_specs=[any_spec] * 4,
        out_specs=(vmem_spec, vmem_spec),
        scratch_shapes=[
            pltpu.VMEM((4, 64), jnp.int32), pltpu.VMEM((4, 32), F32),
            pltpu.VMEM((4, 8, 128, 128), BF16),
            pltpu.VMEM((8, 4, 128, 128), BF16),
            pltpu.VMEM((4, 4, 8, 128), BF16),
            pltpu.VMEM((NW, 1024, LANES), BF16),
            pltpu.VMEM((12, 4, 128), F32),
            pltpu.VMEM((4, 4, 4, 8, 512), F32),
            pltpu.VMEM((NW, 2, 2, 4, 8, LANES), F32),
            pltpu.VMEM((NW, 2, 2, 4, 8, LANES), F32),
            pltpu.VMEM((NW, 2, 2, 4, 8, LANES), F32),
            pltpu.VMEM((NW, 2, 2, 4, 8, LANES), F32),
            pltpu.VMEM((2, 2, 4, 8, 512), F32),
            pltpu.VMEM((2, 2, 8, 512), F32),
            pltpu.VMEM((2, 2, 8, 512), F32),
            pltpu.VMEM((2, 2, 8, 512), F32),
            pltpu.VMEM((2, 2, 8, 512), F32),
            pltpu.VMEM((2, 4, 4, 4, 128), F32),
            pltpu.VMEM((2, 2, 4, 4, 8, 128), BF16),
            pltpu.VMEM((4, 16, 8, 128), F32),
            pltpu.VMEM((15, 4, 8, 128), F32),
            pltpu.VMEM((2, 16, 1, 128), F32),
            pltpu.VMEM((31, 1, 128), F32),
            pltpu.VMEM((1024, 512), BF16),
            dma, dma, dma, dma, dma,
            dma, dma((2,)), dma((2, 8, NW)), dma((NW,)), dma,
            dma((NW, 2, 2)), dma((NW,)), dma, dma,
            dma, dma((2,)), dma, dma,
            pltpu.SemaphoreType.REGULAR, pltpu.SemaphoreType.REGULAR((2,)),
        ],
        compiler_params=pltpu.CompilerParams(
            collective_id=0, has_side_effects=True
        ),
    )(inverse_blocks, lower_blocks, pattern, diag_inverse)
    return column, update


def solution(mesh):
    placed = (
        P("pcol", "prow", None, None),
        P("prow", None, "pcol", None),
        P(),
        P(None, ("prow", "pcol")),
    )
    return jax.shard_map(
        per_device,
        mesh=mesh,
        in_specs=placed,
        out_specs=(P("pcol", None, "prow", None), P(None, ("prow", "pcol"))),
        check_vma=False,
    )
```

```python
import functools

import jax
import jax.numpy as jnp
from jax import lax
from jax.experimental import pallas as pl
from jax.experimental.pallas import tpu as pltpu
from jax.sharding import PartitionSpec as P

MESH = pl.DeviceIdType.MESH
F32 = jnp.float32
BF16 = jnp.bfloat16
TREE = {0: ((3, 3), (1, 1)), 3: ((6, 3), (4, 1), (2, -1)), 6: ((8, 2), (7, 1), (5, -1))}

NW = 2
NN = 4 // NW
LANES = 512 // NW


def kernel(
    inv, low, pat_in, diag_in, col_out, upd_out,
    pat, diag,
    invs, lg, lown, rhs, masks, pbuf, t1, d1, s1, c1, q1, t2, d2, s2, c2, cs, lring, ubuf, urecv, wbuf, wrecv,
    sized, near_send, pass_send, sum_send, low_send, w_send,
    own_sem, pat_sem, ag_recv, pt_recv, low_recv, t1_recv, p1_recv, t2_recv, p2_recv, lr_recv, col_recv, u_recv, w_recv,
    row_sem, col_sem,
):
    p = lax.axis_index("prow")
    z = lax.axis_index("pcol")
    k = lax.rem(p, 2)
    q = lax.div(p, 2)
    x = lax.rem(q, 4)
    y = lax.div(q, 4)
    other = 1 - k

    def dev(yy, xx, kk, zz):
        return (lax.rem(yy + 8, 4) * 8 + lax.rem(xx + 8, 4) * 2 + kk, lax.rem(zz + 32, 16))

    def chip(qq, kk, zz):
        return (qq * 2 + kk, zz)

    partner = dev(y, x, other, z)

    def remote(src, dst, send, recv, to):
        return pltpu.make_async_remote_copy(
            src_ref=src, dst_ref=dst, send_sem=send, recv_sem=recv, device_id=to, device_id_type=MESH
        )

    def await_kib(sem, count):
        ref = sized.at[pl.ds(0, count)]
        pltpu.make_async_copy(ref, ref, sem).wait()

    def signal(sem, to):
        pl.semaphore_signal(sem, inc=1, device_id=to, device_id_type=MESH)

    barrier = pltpu.get_barrier_semaphore()
    near = [partner, dev(y, x + 1, k, z), dev(y, x - 1, k, z), dev(y + 1, x, k, z), dev(y - 1, x, k, z)]
    for hop in range(1, 4):
        near += [dev(y, x, k, z + hop), dev(y, x, k, z - hop)]
    for to in near:
        signal(barrier, to)
    pl.semaphore_wait(barrier, len(near))

    def rows(kk, zz, wave, first=0, count=4):
        return (
            pl.ds(4 * kk + first, count), pl.ds(NN * wave, NN), pl.ds(pl.multiple_of(8 * zz, 8), 8), slice(None)
        )

    def spread(zz, d, way, s, wave, held):
        for t, hop in TREE.get(d, ()):
            first, count = (2 * way, 2) if t == 8 else (0, 4)
            src = lg.at[rows(k, zz, wave, first, count)] if held else low.at[:, pl.ds(NN * wave, NN)]
            c = remote(
                src, lg.at[rows(k, zz, wave, first, count)],
                near_send, ag_recv.at[way, t - 1, wave], dev(y, x, k, z + s * hop),
            )
            yield c

    ways = ((0, 1), (1, -1))
    starts = [[list(spread(z, 0, way, s, wave, False)) for way, s in ways] for wave in range(NW)]
    for hop in range(2):
        for wave in range(NW):
            for way, _ in ways:
                starts[wave][way][hop].start()
    inv_out = remote(
        inv.at[pl.ds(4 * other, 4)], invs.at[:, pl.ds(4 * k, 4)], pass_send, pt_recv.at[0], partner
    )
    whole = (pl.ds(4 * k, 4), slice(None), pl.ds(pl.multiple_of(8 * z, 8), 8), slice(None))
    own_out = remote(low, lg.at[whole], pass_send, pt_recv.at[0], partner)
    own_out.start()
    inv_out.start()
    own_in = pltpu.make_async_copy(low, lg.at[whole], own_sem)
    own_in.start()
    inv_in = pltpu.make_async_copy(inv.at[pl.ds(4 * k, 4)], invs.at[:, pl.ds(4 * k, 4)], own_sem)
    inv_in.start()
    pat_move = pltpu.make_async_copy(pat_in, pat, pat_sem.at[0])
    pat_move.start()
    diag_move = pltpu.make_async_copy(diag_in, diag, pat_sem.at[1])
    diag_move.start()
    root = q == z

    @pl.when(root)
    def _():
        pltpu.make_async_copy(low, lown, low_recv).start()

    signal(row_sem, dev(y, x + 1, k, z))
    signal(row_sem, dev(y, x - 1, k, z))
    pl.semaphore_wait(row_sem, 2)
    for lap in range(2):
        signal(col_sem.at[lap], dev(y + 1, x, k, z))
        signal(col_sem.at[lap], dev(y - 1, x, k, z))
        pl.semaphore_wait(col_sem.at[lap], 2)

    def present(g):
        return jnp.broadcast_to(jnp.sum((pat[...] == g).astype(F32), axis=1, keepdims=True), (4, 128))

    pat_move.wait()
    for j in range(8):
        masks[j] = present(8 * q + j)
    for i in range(4):
        masks[8 + i] = present(8 * z + 4 * k + i)


    def arrive(d, wave):
        for way, s in ways:
            from_z = lax.rem(z - s * d + 32, 16)
            got = lg.at[rows(k, from_z, wave, 2 * way, 2)] if d == 8 else lg.at[rows(k, from_z, wave)]
            pltpu.make_async_copy(got, got, ag_recv.at[way, d - 1, wave]).wait()
            for c in spread(from_z, d, way, s, wave, True):
                c.start()
            c = remote(got, got, pass_send, pt_recv.at[wave], partner)
            c.start()
            if wave == NW - 1 and (d < 8 or way == 1):
                piece = (pl.ds(4 * k, 4), slice(None), pl.ds(pl.multiple_of(8 * from_z, 8), 8), slice(None))
                c = remote(lg.at[piece], lown, low_send, low_recv, chip(from_z, k, z))
                pl.when(root)(c.start)

    order = (3, 1, 6, 4, 2, 7, 5, 8)

    def part(h, i, wave, m):
        lanes = pl.ds(LANES * wave, LANES)
        return pbuf.at[i, :, m, :, lanes] if h == 0 else pbuf.at[i, m, :, :, lanes]

    def mod4(v):
        return lax.rem(v + 8, 4)

    def ring(h, step):
        return (x if (h == 0) == (step == 1) else y)

    def ring_dev(h, step, by):
        return dev(y, x + by, k, z) if (h == 0) == (step == 1) else dev(y + by, x, k, z)

    def begin(h, way, s, step, chunk, t, d, t_sem, sem):
        n = ring(h, step)
        remote(chunk(mod4(n + 2 * s)), t, sum_send, t_sem, ring_dev(h, step, s)).start()
        remote(chunk(mod4(n - s)), d, sum_send, sem, ring_dev(h, step, -s)).start()

    def combine(h, way, s, step, chunk, t, sbuf, cbuf, sem):
        n = ring(h, step)
        sbuf[...] = t[...] + chunk(mod4(n + s))[...]
        remote(sbuf, cbuf, sum_send, sem, ring_dev(h, step, s)).start()

    def finish(h, step, chunk, d, cbuf):
        return chunk(ring(h, step))[...] + d[...] + cbuf[...]

    pairs = [(h, way, s) for way, s in ways for h in range(2)]

    def product(wave):
        for j in range(8):
            for n in range(NN * wave, NN * wave + NN):
                keep = jnp.broadcast_to(masks[j, n : n + 1, :], (128, 128)).astype(BF16)
                rhs[wave, 128 * j : 128 * (j + 1), 128 * (n % NN) : 128 * (n % NN + 1)] = lg[j, n] * keep
        for way, s in ways:
            lhs = jnp.concatenate(
                [jnp.concatenate([invs[2 * h + way, j] for j in range(8)], axis=1) for h in range(2)], axis=0
            )
            prod = jnp.dot(lhs, rhs[wave], preferred_element_type=F32)
            for h in range(2):
                i = 2 * h + way
                pbuf[i, :, :, :, LANES * wave : LANES * (wave + 1)] = prod[128 * h : 128 * (h + 1)].reshape(4, 4, 8, LANES)
                begin(
                    h, way, s, 1, functools.partial(part, h, i, wave),
                    t1.at[wave, h, way], d1.at[wave, h, way], t1_recv.at[wave, h, way], p1_recv.at[wave],
                )

    for d in order[:5]:
        for wave in range(NW):
            arrive(d, wave)
    diag_move.wait()
    for wave in range(NW):
        for d in order[5:]:
            arrive(d, wave)
        if wave == 0:
            await_kib(own_sem, 32 + 512)
        await_kib(pt_recv.at[wave], 30 * 16 // NW + (32 + 512 if wave == 0 else 0))
        product(wave)
    for wave in range(NW):
        for h, way, s in pairs:
            await_kib(t1_recv.at[wave, h, way], 64 // NW)
            combine(
                h, way, s, 1, functools.partial(part, h, 2 * h + way, wave),
                t1.at[wave, h, way], s1.at[wave, h, way], c1.at[wave, h, way], p1_recv.at[wave],
            )

    pltpu.make_async_copy(lown, lown, low_recv).wait()
    mine = (y, x)
    for h in range(2):
        c = pltpu.make_async_copy(lown.at[pl.ds(2 * h, 2)], lring.at[h, :, mine[h]], lr_recv)
        c.start()
        for by in (2, 1, 3):
            to = dev(y + by, x, k, z) if h == 0 else dev(y, x + by, k, z)
            c = remote(lown.at[pl.ds(2 * h, 2)], lring.at[h, :, mine[h]], near_send, lr_recv, to)
            c.start()
    for wave in range(NW):
        await_kib(p1_recv.at[wave], 512 // NW)
    for h, way, s in pairs:
        for wave in range(NW):
            q1[h, way, :, :, LANES * wave : LANES * (wave + 1)] = finish(
                h, 1, functools.partial(part, h, 2 * h + way, wave), d1.at[wave, h, way], c1.at[wave, h, way]
            )
        begin(
            h, way, s, 2, lambda m, h=h, way=way: q1.at[h, way, m], t2.at[h, way], d2.at[h, way], t2_recv, p2_recv
        )
    await_kib(lr_recv, 128)
    for n in range(4):
        left = lring[:, :, :, n].astype(F32).reshape(128, 128).astype(BF16)
        right = jnp.concatenate(
            [
                -jnp.broadcast_to(masks[8 + 2 * h + way, n : n + 1, :], (32, 128))
                * q1[h, way, :, :, 128 * n : 128 * (n + 1)].reshape(32, 128)
                for h in range(2)
                for way in range(2)
            ],
            axis=0,
        )
        prod = jnp.zeros((128, 128), F32)
        for _ in range(3):
            taken = right.astype(BF16)
            prod = prod + lax.dot_general(left, taken, (((0,), (0,)), ((), ())), preferred_element_type=F32)
            right = right - taken.astype(F32)
        ubuf[n] = prod.reshape(16, 8, 128)

    def u_copy(dy, dx):
        to_y, to_x = mod4(y + dy), mod4(x + dx)
        slot = 4 * dy + dx - 1
        return remote(
            ubuf.at[:, 4 * to_y + to_x], urecv.at[slot], near_send, u_recv, dev(to_y, to_x, k, z)
        )

    far = (0, 1, 2, 1)
    u_order = sorted(((dy, dx) for dy in range(4) for dx in range(4) if dy + dx), key=lambda v: -far[v[0]] - far[v[1]])
    u_sends = [u_copy(dy, dx) for dy, dx in u_order]
    for c in u_sends:
        c.start()

    await_kib(t2_recv, 64)
    for h, way, s in pairs:
        combine(h, way, s, 2, lambda m, h=h, way=way: q1.at[h, way, m],
            t2.at[h, way], s2.at[h, way], c2.at[h, way], p2_recv)
    value = ubuf[:, q]
    await_kib(u_recv, 240)
    for slot in range(15):
        value = value + urecv[slot]

    group = lax.broadcasted_iota(jnp.int32, (8, 128), 1) // 32
    for m in range(4):
        packed = jnp.zeros((8, 128), F32)
        for n in range(4):
            turned = value[n] if n == m else pltpu.roll(value[n], (32 * (n - m)) % 128, 1)
            packed = jnp.where(group == n, turned, packed)
        for r in range(8):
            wbuf[r // 4, 4 * (r % 4) + m] = packed[r : r + 1, :]

    def w_copy(flip, step):
        kk = k if flip == 0 else other
        zz = lax.rem(z + step, 16)
        return remote(
            wbuf.at[kk, zz], wrecv.at[16 * flip + step - 1], w_send, w_recv, chip(q, kk, zz)
        )

    w_order = [(flip, step) for step in sorted(range(1, 16), key=lambda v: -min(v, 16 - v)) for flip in range(2)] + [(1, 0)]
    w_sends = [w_copy(flip, step) for flip, step in w_order]
    for c in w_sends:
        c.start()

    await_kib(p2_recv, 128)
    columns = [None] * 4
    for h, way, s in pairs:
        i = 2 * h + way
        total = finish(h, 2, lambda m, h=h, way=way: q1.at[h, way, m],
            d2.at[h, way], c2.at[h, way])
        keep_row = jnp.concatenate(
            [jnp.broadcast_to(masks[8 + i, n : n + 1, :], (8, 128)) for n in range(4)], axis=1
        )
        columns[i] = -keep_row * total

    for half in range(2):
        for i in range(4):
            for n in range(4):
                cs[half, i, n] = columns[i][4 * half : 4 * half + 4, 128 * n : 128 * (n + 1)]
    col_move = pltpu.make_async_copy(cs.at[k], col_out.at[pl.ds(4 * k, 4)], col_recv.at[0])
    col_move.start()
    col_pass = remote(cs.at[other], col_out.at[pl.ds(4 * k, 4)], near_send, col_recv.at[1], partner)
    col_pass.start()

    await_kib(near_send, 480 + 96 + 240 + 32)
    await_kib(pass_send, 512 + 512)
    await_kib(sum_send, 768 + 192)

    @pl.when(root)
    def _():
        await_kib(low_send, 480)

    col_move.wait()
    col_pass.wait_recv()

    pltpu.make_async_copy(wrecv, wrecv, w_recv).wait()
    total = wbuf[k, z]
    for slot in range(31):
        total = total + wrecv[slot]
    for n in range(4):
        upd_out[n : n + 1, :] = diag[n : n + 1, :] - total[:, 32 * n : 32 * (n + 1)]
    pltpu.make_async_copy(wrecv, wrecv, w_send).wait()


def per_device(inverse_blocks, lower_blocks, pattern, diag_inverse):
    any_spec = pl.BlockSpec(memory_space=pltpu.HBM)
    vmem_spec = pl.BlockSpec(memory_space=pltpu.VMEM)
    dma = pltpu.SemaphoreType.DMA
    column, update = pl.pallas_call(
        kernel,
        out_shape=(
            pltpu.VMEM((8, 4, 4, 128), F32),
            pltpu.VMEM((4, 32), F32),
        ),
        in_specs=[any_spec] * 4,
        out_specs=(vmem_spec, vmem_spec),
        scratch_shapes=[
            pltpu.VMEM((4, 64), jnp.int32), pltpu.VMEM((4, 32), F32),
            pltpu.VMEM((4, 8, 128, 128), BF16),
            pltpu.VMEM((8, 4, 128, 128), BF16),
            pltpu.VMEM((4, 4, 8, 128), BF16),
            pltpu.VMEM((NW, 1024, LANES), BF16),
            pltpu.VMEM((12, 4, 128), F32),
            pltpu.VMEM((4, 4, 4, 8, 512), F32),
            pltpu.VMEM((NW, 2, 2, 4, 8, LANES), F32),
            pltpu.VMEM((NW, 2, 2, 4, 8, LANES), F32),
            pltpu.VMEM((NW, 2, 2, 4, 8, LANES), F32),
            pltpu.VMEM((NW, 2, 2, 4, 8, LANES), F32),
            pltpu.VMEM((2, 2, 4, 8, 512), F32),
            pltpu.VMEM((2, 2, 8, 512), F32),
            pltpu.VMEM((2, 2, 8, 512), F32),
            pltpu.VMEM((2, 2, 8, 512), F32),
            pltpu.VMEM((2, 2, 8, 512), F32),
            pltpu.VMEM((2, 4, 4, 4, 128), F32),
            pltpu.VMEM((2, 2, 4, 4, 8, 128), BF16),
            pltpu.VMEM((4, 16, 8, 128), F32),
            pltpu.VMEM((15, 4, 8, 128), F32),
            pltpu.VMEM((2, 16, 1, 128), F32),
            pltpu.VMEM((31, 1, 128), F32),
            pltpu.VMEM((1024, 512), BF16),
            dma, dma, dma, dma, dma,
            dma, dma((2,)), dma((2, 8, NW)), dma((NW,)), dma,
            dma((NW, 2, 2)), dma((NW,)), dma, dma,
            dma, dma((2,)), dma, dma,
            pltpu.SemaphoreType.REGULAR, pltpu.SemaphoreType.REGULAR((2,)),
        ],
        compiler_params=pltpu.CompilerParams(
            collective_id=0, has_side_effects=True
        ),
    )(inverse_blocks, lower_blocks, pattern, diag_inverse)
    return column, update


def solution(mesh):
    placed = (
        P("pcol", "prow", None, None),
        P("prow", None, "pcol", None),
        P(),
        P(None, ("prow", "pcol")),
    )
    return jax.shard_map(
        per_device,
        mesh=mesh,
        in_specs=placed,
        out_specs=(P("pcol", None, "prow", None), P(None, ("prow", "pcol"))),
        check_vma=False,
    )
```
